32 devices in a mesh: rows: 8 (over z, x), cols: 4 (over y, core).
Axes of the slice: x: 2, y: 2, z: 4, core: 2. Of those that a mesh axis runs over, the one named last changes fastest.
Arguments:
- query: bfloat16 [24, 256, 2048], P('rows', 'cols'), may hold values from -6 to 6
- key: bfloat16 [24, 256, 2048], P('rows', 'cols'), may hold values from -6 to 6
- value: bfloat16 [24, 256, 2048], P('rows', 'cols'), may hold values from -6 to 6
- cotangent: bfloat16 [24, 256, 2048], P('rows', 'cols'), may hold values from -6 to 6
- conv_weight: bfloat16 [9, 2048], replicated, may hold values from -1.1953125 to 1.1953125
- row_mask: int32 [24, 2, 2], P('rows'), may hold values from 0 to 1, as said below
- col_mask: int32 [256, 3, 3], P('cols'), may hold values from 0 to 1, as said below
Outputs:
- out: bfloat16 [24, 256, 2048], P('rows', 'cols')
- dquery: bfloat16 [24, 256, 2048], P('rows', 'cols')
- dkey: bfloat16 [24, 256, 2048], P('rows', 'cols')
- dvalue: bfloat16 [24, 256, 2048], P('rows', 'cols')
The draws below stay inside these ranges and needn't reach their ends.
Inputs may be any that keep to these rules, and one draw needn't show every extreme that they name: `row_mask`: every diagonal block is 1: a query block always sees its own block. `col_mask`: every diagonal block is 1: a query block always sees its own block.
All inputs are finite; a program needn't handle non-finite values.
Results may differ from the reference program's by a relative error of at most 0.011.
Values may be sent and summed in bfloat16 or wider, within the bound.
A program may use at most 128 MiB of HBM per device.

```python
import math
import jax
import jax.numpy as jnp
from jax import lax

D = 2048
HEAD_DIM = 128
SHEET_ROW_BLOCKS = 2
COL_BLOCKS = 3
SHEET_ROWS = 24
SHEET_COLS = 256


def draw_query(key, part):
    base = jax.random.normal(jax.random.fold_in(key, 1), (SHEET_ROWS, SHEET_COLS, D), jnp.float32)
    return jnp.clip(base, -6.0, 6.0).astype(jnp.bfloat16)


def draw_key(key, part):
    base = jax.random.normal(jax.random.fold_in(key, 4), (SHEET_ROWS, SHEET_COLS, D), jnp.float32)
    return jnp.clip(base, -6.0, 6.0).astype(jnp.bfloat16)


def block_mask_table(key, lines, blocks):
    flips = jax.random.randint(key, (lines, blocks, blocks), 0, 2)
    diagonal = lax.broadcasted_iota(jnp.int32, (1, blocks, blocks), 1) == lax.broadcasted_iota(jnp.int32, (1, blocks, blocks), 2)
    return jnp.where(diagonal, 1, flips).astype(jnp.int32)


def draw_row_mask(key, part):
    return block_mask_table(jax.random.fold_in(key, 21), SHEET_ROWS, SHEET_ROW_BLOCKS)


def draw_col_mask(key, part):
    return block_mask_table(jax.random.fold_in(key, 22), SHEET_COLS, COL_BLOCKS)


def block_levels(rng, dims, shards, low, largest):
    gain, own = 1.0, jax.random.fold_in(rng, 6)
    for position, shards_of in shards:
        heights = jnp.exp(jax.random.uniform(jax.random.fold_in(own, position), (shards_of,), jnp.float32, low / len(shards), largest / len(shards)))
        gain = gain * jnp.repeat(heights, dims[position] // shards_of).reshape([-1 if axis == position else 1 for axis in range(len(dims))])
    return gain


def bell_draw(own_key, extent, deviation, most, cuts=(), held_as=jnp.bfloat16):
    gain = block_levels(own_key, extent, cuts, -0.22, 0.18) if cuts else 1.0
    entries = jax.random.normal(own_key, extent, jnp.float32) * deviation * gain
    return jnp.minimum(jnp.maximum(entries, -most), most).astype(held_as)


def setup_inputs(seed: int = 0) -> dict:
    arg_keys = jax.random.split(jax.random.key(seed), 8)
    return {
        "query": draw_query(jax.random.fold_in(arg_keys[7], 71), 0),
        "key": draw_key(jax.random.fold_in(arg_keys[7], 71), 0),
        "value": bell_draw(arg_keys[2], (SHEET_ROWS, SHEET_COLS, D), 1.0, 6.0, ((0, 8), (1, 4))),
        "cotangent": bell_draw(arg_keys[3], (SHEET_ROWS, SHEET_COLS, D), 1.0, 6.0, ((0, 8), (1, 4))),
        "conv_weight": bell_draw(arg_keys[4], (9, D), 0.3, 1.1953125),
        "row_mask": draw_row_mask(jax.random.fold_in(arg_keys[7], 71), 0),
        "col_mask": draw_col_mask(jax.random.fold_in(arg_keys[7], 71), 0),
    }


def attend_line(query_line, key_line, value_line, grad_line, allowed):
    score_scale = 1.0 / math.sqrt(HEAD_DIM)
    query_full = query_line.astype(jnp.float32)
    key_full = key_line.astype(jnp.float32)
    value_full = value_line.astype(jnp.float32)
    grad_full = grad_line.astype(jnp.float32)
    scores = jnp.einsum('qhd,khd->hqk', query_full, key_full) * score_scale
    scores = jnp.where(allowed[None], scores, -jnp.inf)
    highest = lax.optimization_barrier(jnp.max(scores, axis=-1, keepdims=True))
    weights = jnp.exp(scores - highest)
    weights = weights / lax.optimization_barrier(jnp.sum(weights, axis=-1, keepdims=True))
    rounded = lax.optimization_barrier(weights.astype(jnp.bfloat16)).astype(jnp.float32)
    attended = jnp.einsum('hqk,khd->qhd', rounded, value_full)
    dweights = jnp.einsum('qhd,khd->hqk', grad_full, value_full)
    delta = jnp.transpose(lax.optimization_barrier(jnp.sum(grad_full * attended, axis=-1)), (1, 0))
    dscores = (weights * (dweights - delta[:, :, None]) * score_scale).astype(jnp.bfloat16)
    dscores = lax.optimization_barrier(dscores).astype(jnp.float32)
    dquery = jnp.einsum('hqk,khd->qhd', dscores, key_full)
    dkey = jnp.einsum('hqk,qhd->khd', dscores, query_full)
    dvalue = jnp.einsum('hqk,qhd->khd', rounded, grad_full)
    return (attended.astype(jnp.bfloat16), dquery.astype(jnp.bfloat16), dkey.astype(jnp.bfloat16), dvalue.astype(jnp.bfloat16))

def depthwise_sheet(field, taps, reverse_taps):
    padded = jnp.pad(field, ((1, 1), (1, 1), (0, 0)))

    def one_row(index):
        window = lax.dynamic_slice_in_dim(padded, index.astype(jnp.int32), 3, 0).astype(jnp.float32)
        summed = jnp.zeros((SHEET_COLS, D), jnp.float32)
        for row_offset_start in range(3):
            for offset_col in range(3):
                if reverse_taps:
                    start_row = 2 - row_offset_start
                    start_col = 2 - offset_col
                else:
                    start_row = row_offset_start
                    start_col = offset_col
                picked = window[start_row, start_col:start_col + SHEET_COLS]
                summed = summed + taps[row_offset_start * 3 + offset_col] * picked
        return summed
    return lax.map(one_row, jnp.arange(SHEET_ROWS, dtype=jnp.int32))

def run_line(items):
    return attend_line(items[0], items[1], items[2], items[3], items[4])

def reference(query, key, value, cotangent, conv_weight, row_mask, col_mask):
    half_width = D // 2
    head_count = half_width // HEAD_DIM
    shaped = [x.reshape(SHEET_ROWS, SHEET_COLS, 2, head_count, HEAD_DIM) for x in (query, key, value, cotangent)]
    row_parts = tuple((x[:, :, 0] for x in shaped))
    col_parts = tuple((jnp.transpose(x[:, :, 1], (1, 0, 2, 3)) for x in shaped))
    row_len = SHEET_COLS // SHEET_ROW_BLOCKS
    row_allowed = jnp.repeat(jnp.repeat(row_mask, row_len, axis=1), row_len, axis=2) == 1
    col_len = SHEET_ROWS // COL_BLOCKS
    col_allowed = jnp.repeat(jnp.repeat(col_mask, col_len, axis=1), col_len, axis=2) == 1
    row_results = lax.map(run_line, row_parts + (row_allowed,))
    col_results = lax.map(run_line, col_parts + (col_allowed,))

    def assemble(row_piece, col_piece):
        joined = jnp.stack([row_piece, jnp.transpose(col_piece, (1, 0, 2, 3))], axis=2)
        return lax.optimization_barrier(joined.reshape(SHEET_ROWS, SHEET_COLS, D))
    attended16 = assemble(row_results[0], col_results[0])
    dquery = assemble(row_results[1], col_results[1])
    dkey = assemble(row_results[2], col_results[2])
    dvalue_attn = assemble(row_results[3], col_results[3])
    taps = conv_weight.astype(jnp.float32)
    lepe = depthwise_sheet(value, taps, False)
    out = (attended16.astype(jnp.float32) + lepe).astype(jnp.bfloat16)
    dvalue = (dvalue_attn.astype(jnp.float32) + depthwise_sheet(cotangent, taps, True)).astype(jnp.bfloat16)
    return (out, dquery, dkey, dvalue)
```

```python
import functools
import math

import jax
import jax.numpy as jnp
from jax import lax
from jax.experimental import pallas as pl
from jax.experimental.pallas import tpu as pltpu
from jax.sharding import PartitionSpec as P

HEAD_DIM = 128
SHEET_ROW_BLOCKS = 2
COL_BLOCKS = 3


def padded(array, sides, width):
    for axis, dim in sides:
        devices, length = (lax.axis_size(axis), array.shape[dim])
        up = [(i, (i + 1) % devices) for i in range(devices - 1)]
        down = [(j, i) for i, j in up]
        last = lax.slice_in_dim(array, length - width, length, axis=dim)
        leading = lax.slice_in_dim(array, 0, width, axis=dim)
        before = lax.ppermute(last, axis, up)
        after = lax.ppermute(leading, axis, down)
        array = jnp.concatenate([before, array, after], axis=dim)
    return array


def block_allow(block_mask_table, query_pos, key_pos, block_len, block_count):
    labels = jnp.arange(block_count)
    query_onehot_rows = (query_pos[:, None] // block_len == labels[None, :]).astype(jnp.float32)
    key_onehot_rows = (key_pos[:, None] // block_len == labels[None, :]).astype(jnp.float32)
    merged_links = jnp.einsum(
        "xv,zvs,hs->zxh", query_onehot_rows, block_mask_table.astype(jnp.float32), key_onehot_rows
    )
    return merged_links > 0.5


def line_attention(query_part, key_part, value_part, grad_part, allowed, layout):
    if layout == "bq":
        query_form = "bqhd"
        key_layout_shape = "bkhd"
    else:
        query_form = "qbhd"
        key_layout_shape = "kbhd"
    score_scale = 1.0 / math.sqrt(query_part.shape[-1])
    pair_form = query_form + "," + key_layout_shape + "->bhqk"
    scores = (
        jnp.einsum(pair_form, query_part, key_part, preferred_element_type=jnp.float32)
        * score_scale
    )
    scores = jnp.where(allowed[:, None], scores, -jnp.inf)
    highest = jnp.max(scores, axis=-1, keepdims=True)
    weights = jnp.exp(scores - highest)
    weights = weights / jnp.sum(weights, axis=-1, keepdims=True)
    rounded = weights.astype(jnp.bfloat16)
    attended = jnp.einsum(
        "bhqk," + key_layout_shape + "->" + query_form,
        rounded,
        value_part,
        preferred_element_type=jnp.float32,
    )
    dweights = jnp.einsum(pair_form, grad_part, value_part, preferred_element_type=jnp.float32)
    delta = jnp.sum(grad_part.astype(jnp.float32) * attended, axis=-1)
    if layout == "bq":
        delta = jnp.transpose(delta, (0, 2, 1))
    else:
        delta = jnp.transpose(delta, (1, 2, 0))
    dscores = (weights * (dweights - delta[..., None]) * score_scale).astype(jnp.bfloat16)
    dquery = jnp.einsum(
        "bhqk," + key_layout_shape + "->" + query_form,
        dscores,
        key_part,
        preferred_element_type=jnp.float32,
    )
    dkey = jnp.einsum(
        "bhqk," + query_form + "->" + key_layout_shape,
        dscores,
        query_part,
        preferred_element_type=jnp.float32,
    )
    dvalue = jnp.einsum(
        "bhqk," + query_form + "->" + key_layout_shape,
        rounded,
        grad_part,
        preferred_element_type=jnp.float32,
    )
    return (attended, dquery, dkey, dvalue)


def depthwise(padded_field, taps, rows_count, cols_count, reverse_taps):
    summed = jnp.zeros((rows_count, cols_count, taps.shape[1]), jnp.float32)
    for row_offset_start in range(3):
        for offset_col in range(3):
            if reverse_taps:
                start_row = 2 - row_offset_start
                start_col = 2 - offset_col
            else:
                start_row = row_offset_start
                start_col = offset_col
            window = padded_field[
                start_row : start_row + rows_count, start_col : start_col + cols_count
            ]
            summed = summed + taps[row_offset_start * 3 + offset_col] * window.astype(jnp.float32)
    return summed


def body(query, key, value, cotangent, conv_weight, row_mask, col_mask):
    rows_here, cols_here, width = query.shape
    half_width = width // 2
    head_groups = half_width // HEAD_DIM
    row_devices = lax.axis_size("rows")
    col_devices = lax.axis_size("cols")
    sheet_rows = rows_here * row_devices
    sheet_cols = cols_here * col_devices
    taps = conv_weight.astype(jnp.float32)
    padded_value = padded(value, (("rows", 0), ("cols", 1)), 1)
    padded_grad = padded(cotangent, (("rows", 0), ("cols", 1)), 1)
    row_len = sheet_cols // SHEET_ROW_BLOCKS
    keys_row, values_row = (
        lax.all_gather(key[:, :, :half_width], "cols", axis=1, tiled=True),
        lax.all_gather(value[:, :, :half_width], "cols", axis=1, tiled=True),
    )
    col_start = lax.axis_index("cols") * cols_here
    allowed = block_allow(
        row_mask,
        col_start + jnp.arange(cols_here),
        jnp.arange(sheet_cols),
        row_len,
        SHEET_ROW_BLOCKS,
    )
    local_shape = (rows_here, cols_here, head_groups, HEAD_DIM)
    whole_shape = (rows_here, sheet_cols, head_groups, HEAD_DIM)
    results = line_attention(
        query[:, :, :half_width].reshape(local_shape),
        keys_row.reshape(whole_shape),
        values_row.reshape(whole_shape),
        cotangent[:, :, :half_width].reshape(local_shape),
        allowed,
        "bq",
    )
    key_terms = results[2].reshape(rows_here, sheet_cols, half_width)
    value_terms = results[3].reshape(rows_here, sheet_cols, half_width)
    key_grads, value_grads = (
        lax.psum_scatter(key_terms, "cols", scatter_dimension=1, tiled=True),
        lax.psum_scatter(value_terms, "cols", scatter_dimension=1, tiled=True),
    )
    out_row = results[0].reshape(rows_here, cols_here, half_width).astype(jnp.bfloat16)
    dq_row = results[1].reshape(rows_here, cols_here, half_width).astype(jnp.bfloat16)
    dk_row = key_grads.astype(jnp.bfloat16)
    dv_row = value_grads.astype(jnp.bfloat16)
    columns_each = cols_here // row_devices
    moved = (
        lax.all_to_all(query[:, :, half_width:], "rows", split_axis=1, concat_axis=0, tiled=True),
        lax.all_to_all(key[:, :, half_width:], "rows", split_axis=1, concat_axis=0, tiled=True),
        lax.all_to_all(value[:, :, half_width:], "rows", split_axis=1, concat_axis=0, tiled=True),
        lax.all_to_all(
            cotangent[:, :, half_width:], "rows", split_axis=1, concat_axis=0, tiled=True
        ),
    )
    column_shape = (sheet_rows, columns_each, head_groups, HEAD_DIM)
    my_tables = lax.dynamic_slice_in_dim(
        col_mask, lax.axis_index("rows") * columns_each, columns_each, 0
    )
    col_len = sheet_rows // COL_BLOCKS
    positions = jnp.arange(sheet_rows)
    col_allowed = block_allow(my_tables, positions, positions, col_len, COL_BLOCKS)
    col_results = line_attention(
        moved[0].reshape(column_shape),
        moved[1].reshape(column_shape),
        moved[2].reshape(column_shape),
        moved[3].reshape(column_shape),
        col_allowed,
        "qb",
    )
    column_flat = (sheet_rows, columns_each, half_width)
    col_pieces = [piece.reshape(column_flat).astype(jnp.bfloat16) for piece in col_results]
    out_col, dq_col, dk_col, dv_col = (
        lax.all_to_all(col_pieces[0], "rows", split_axis=0, concat_axis=1, tiled=True),
        lax.all_to_all(col_pieces[1], "rows", split_axis=0, concat_axis=1, tiled=True),
        lax.all_to_all(col_pieces[2], "rows", split_axis=0, concat_axis=1, tiled=True),
        lax.all_to_all(col_pieces[3], "rows", split_axis=0, concat_axis=1, tiled=True),
    )
    lepe = depthwise(padded_value, taps, rows_here, cols_here, False)
    back_conv = depthwise(padded_grad, taps, rows_here, cols_here, True)
    attended16 = jnp.concatenate([out_row, out_col], axis=2)
    out = (attended16.astype(jnp.float32) + lepe).astype(jnp.bfloat16)
    dquery = jnp.concatenate([dq_row, dq_col], axis=2)
    dkey = jnp.concatenate([dk_row, dk_col], axis=2)
    dvalue_attn = jnp.concatenate([dv_row, dv_col], axis=2)
    dvalue = (dvalue_attn.astype(jnp.float32) + back_conv).astype(jnp.bfloat16)
    return (out, dquery, dkey, dvalue)


SUB = 8
CHUNKS = 2
MESH = pl.DeviceIdType.MESH


def attend(q, k, v, g, allow):
    scale = 1.0 / math.sqrt(HEAD_DIM)
    nt = (((1,), (1,)), ((), ()))
    nn = (((1,), (0,)), ((), ()))
    tn = (((0,), (0,)), ((), ()))
    dot = functools.partial(lax.dot_general, preferred_element_type=jnp.float32)
    s = jnp.where(allow, dot(q, k, nt) * scale, -jnp.inf)
    e = jnp.exp(s - jnp.max(s, axis=-1, keepdims=True))
    w = e * (1.0 / jnp.sum(e, axis=-1, keepdims=True))
    w16 = w.astype(jnp.bfloat16)
    att = dot(w16, v, nn)
    dw = dot(g, v, nt)
    delta = jnp.sum(g.astype(jnp.float32) * att, axis=-1, keepdims=True)
    ds = (w * (dw - delta) * scale).astype(jnp.bfloat16)
    return att, dot(ds, k, nn), dot(ds, q, tn), dot(w16, g, tn)


def layer_kernel(
    dims, q_hbm, k_hbm, v_hbm, g_hbm, taps, row_allow, col_allow, *rest
):
    R, C, rows, groups, width = dims
    outs_hbm = rest[:4]
    colbuf, colout, rowbuf, rowout, ext, conv, ret, done = rest[4:12]
    (ci_s, ci_r, co_s, co_r, ri_s, ri_r, ro_s, ro_r, ha_s, ha_r, local, final) = rest[12:]
    half = width // 2
    share = half // C
    part = half // CHUNKS
    me = lax.axis_index("rows")
    mc = lax.axis_index("cols")
    inputs = (q_hbm, k_hbm, v_hbm, g_hbm)
    f32 = jnp.float32

    def lanes(start, size):
        return pl.ds(pl.multiple_of(start, 128), size)

    def col_in(t, ch, p, slot):
        return pltpu.make_async_remote_copy(
            src_ref=inputs[t].at[:, p, :, pl.ds(half + ch * part, part)],
            dst_ref=colbuf.at[t, slot, :, :, pl.ds(ch * part, part)],
            send_sem=ci_s.at[t, ch, p], recv_sem=ci_r.at[t, ch, slot],
            device_id={"rows": p}, device_id_type=MESH)

    def col_back(t, ch, p, slot):
        return pltpu.make_async_remote_copy(
            src_ref=colout.at[t, p, :, :, pl.ds(ch * part, part)],
            dst_ref=ret.at[t, :, slot, :, pl.ds(half + ch * part, part)],
            send_sem=co_s.at[t, ch, p], recv_sem=co_r.at[t, ch, slot],
            device_id={"rows": p}, device_id_type=MESH)

    def row_in(t, p, slot):
        return pltpu.make_async_remote_copy(
            src_ref=inputs[t].at[:, :, :, lanes(p * share, share)],
            dst_ref=rowbuf.at[t, :, slot],
            send_sem=ri_s.at[t, p], recv_sem=ri_r.at[t, slot],
            device_id={"cols": p}, device_id_type=MESH)

    def row_back(t, p, slot):
        return pltpu.make_async_remote_copy(
            src_ref=rowout.at[t, :, p],
            dst_ref=ret.at[t, :, :, :, lanes(slot * share, share)],
            send_sem=ro_s.at[t, p], recv_sem=ro_r.at[t, slot],
            device_id={"cols": p}, device_id_type=MESH)

    def row_span(dr, there):
        if dr == 0:
            return pl.ds(1, rows) if there else pl.ds(0, rows)
        if dr == 1:
            return pl.ds(0, 1) if there else pl.ds(rows - 1, 1)
        return pl.ds(rows + 1, 1) if there else pl.ds(0, 1)

    def group_span(dc, there):
        if dc == 0:
            return pl.ds(1, groups) if there else pl.ds(0, groups)
        if dc == 1:
            return pl.ds(0, 1) if there else pl.ds(groups - 1, 1)
        return pl.ds(groups + 1, 1) if there else pl.ds(0, 1)

    directions = [(a, b) for a in (-1, 0, 1) for b in (-1, 0, 1) if (a, b) != (0, 0)]

    def halo(t, i):
        dr, dc = directions[i]
        return pltpu.make_async_remote_copy(
            src_ref=inputs[2 + t].at[row_span(dr, False), group_span(dc, False)],
            dst_ref=ext.at[t, row_span(dr, True), group_span(dc, True)],
            send_sem=ha_s.at[t, i], recv_sem=ha_r.at[t, i],
            device_id={"rows": me + dr, "cols": mc + dc}, device_id_type=MESH)

    def has(i, sign):
        dr, dc = directions[i]
        conds = []
        if sign * dr == 1:
            conds.append(me < R - 1)
        if sign * dr == -1:
            conds.append(me > 0)
        if sign * dc == 1:
            conds.append(mc < C - 1)
        if sign * dc == -1:
            conds.append(mc > 0)
        ok = conds[0]
        for c in conds[1:]:
            ok = jnp.logical_and(ok, c)
        return ok

    barrier = pltpu.get_barrier_semaphore()
    for d in range(1, R):
        pl.semaphore_signal(barrier, inc=1, device_id={"rows": lax.rem(me + d, R)}, device_id_type=MESH)
    for d in range(1, C):
        pl.semaphore_signal(barrier, inc=1, device_id={"cols": lax.rem(mc + d, C)}, device_id_type=MESH)
    for dr, dc in ((1, 1), (1, -1), (-1, 1), (-1, -1)):
        corner = {"rows": lax.rem(me + dr + R, R), "cols": lax.rem(mc + dc + C, C)}
        pl.semaphore_signal(barrier, inc=1, device_id=corner, device_id_type=MESH)
    pl.semaphore_wait(barrier, R - 1 + C - 1 + 4)

    order = sorted(range(1, R), key=lambda d: abs(d - R / 2))
    col_order = sorted(range(1, C), key=lambda d: abs(d - C / 2))
    for d in col_order:
        for t in range(4):
            row_in(t, lax.rem(mc + d, C), mc).start()
    for ch in range(CHUNKS):
        for d in order:
            for t in range(4):
                col_in(t, ch, lax.rem(me + d, R), me).start()
    for t in range(2):
        for i in range(8):
            @pl.when(has(i, 1))
            def _(t=t, i=i):
                halo(t, i).start()

    mine = []
    for t in range(4):
        mine.append(pltpu.make_async_copy(inputs[t].at[:, :, :, lanes(mc * share, share)], rowbuf.at[t, :, mc], local.at[0, t]))
        mine.append(pltpu.make_async_copy(inputs[t].at[:, me, :, pl.ds(half, half)], colbuf.at[t, me], local.at[1, t]))
    for t in range(2):
        mine.append(pltpu.make_async_copy(inputs[2 + t], ext.at[t, pl.ds(1, rows), pl.ds(1, groups)], local.at[2, t]))
    for c in mine:
        c.start()
    for t in range(2):
        for i in range(8):
            @pl.when(jnp.logical_not(has(i, -1)))
            def _(t=t, i=i):
                dr, dc = directions[i]
                view = ext.at[t, row_span(dr, True), group_span(dc, True)]
                view[...] = jnp.zeros(view.shape, view.dtype)
    for c in mine:
        c.wait()

    for d in col_order:
        for t in range(4):
            p = lax.rem(mc + d, C)
            row_in(t, p, p).wait_recv()
    tokens = C * groups * SUB

    def row_step(n, carry):
        i, h = n // (share // HEAD_DIM), lax.rem(n, share // HEAD_DIM)
        cols = lanes(h * HEAD_DIM, HEAD_DIM)
        x = [rowbuf[t, i, :, :, :, cols].astype(f32).reshape(tokens, HEAD_DIM).astype(jnp.bfloat16) for t in range(4)]
        table = row_allow[i]
        size = tokens // SHEET_ROW_BLOCKS
        allow = jnp.concatenate(
            [jnp.broadcast_to(table[b : b + 1], (size, tokens)) for b in range(SHEET_ROW_BLOCKS)], axis=0) > 0.5
        for t, y in enumerate(attend(*x, allow)):
            rowout[t, i, :, :, :, cols] = y.reshape(C, groups, SUB, HEAD_DIM).astype(jnp.bfloat16)
        return carry

    lax.fori_loop(0, rows * (share // HEAD_DIM), row_step, 0)
    for d in col_order:
        for t in range(4):
            row_back(t, lax.rem(mc + d, C), mc).start()
    mine = [pltpu.make_async_copy(rowout.at[t, :, mc], ret.at[t, :, :, :, lanes(mc * share, share)], local.at[0, t]) for t in range(4)]
    for c in mine:
        c.start()

    length = R * rows * SUB
    col_size = length // COL_BLOCKS
    for ch in range(CHUNKS):
        for d in order:
            for t in range(4):
                p = lax.rem(me + d, R)
                col_in(t, ch, p, p).wait_recv()
        allow = jnp.concatenate(
            [jnp.broadcast_to(col_allow[b][None], (col_size // SUB, SUB, length)).reshape(col_size, length) for b in range(COL_BLOCKS)], axis=0) > 0.5

        def col_step(h, carry):
            cols = lanes(ch * part + h * HEAD_DIM, HEAD_DIM)
            x = [colbuf[t, :, :, :, cols].astype(f32).reshape(length, HEAD_DIM).astype(jnp.bfloat16) for t in range(4)]
            for t, y in enumerate(attend(*x, allow)):
                colout[t, :, :, :, cols] = y.reshape(R, rows, SUB, HEAD_DIM).astype(jnp.bfloat16)
            return carry

        lax.fori_loop(0, part // HEAD_DIM, col_step, 0)
        for d in order:
            for t in range(4):
                col_back(t, ch, lax.rem(me + d, R), me).start()
    own = [pltpu.make_async_copy(colout.at[t, me], ret.at[t, :, me, :, pl.ds(half, half)], local.at[1, t]) for t in range(4)]
    for c in own:
        c.start()

    for t in range(2):
        for i in range(8):
            @pl.when(has(i, -1))
            def _(t=t, i=i):
                pltpu.make_async_remote_copy(
                    src_ref=inputs[2 + t].at[row_span(directions[i][0], False), group_span(directions[i][1], False)],
                    dst_ref=ext.at[t, row_span(directions[i][0], True), group_span(directions[i][1], True)],
                    send_sem=ha_s.at[t, i], recv_sem=ha_r.at[t, i],
                    device_id={"rows": me - directions[i][0], "cols": mc - directions[i][1]}, device_id_type=MESH).wait_recv()
    long = groups * SUB

    def conv_step(n, carry):
        cols = lanes(n * 128, 128)
        weights = taps[:, cols].astype(f32)
        for t in range(2):
            sums = [None] * rows
            for r in range(rows + 2):
                line = ext[t, r, :, :, cols].astype(f32).reshape(long + 2 * SUB, 128)
                for b in range(3):
                    seen = line[SUB + b - 1 : SUB + b - 1 + long]
                    for a in range(3):
                        o = r - a
                        if 0 <= o < rows:
                            tap = 3 * a + b if t == 0 else 8 - 3 * a - b
                            term = weights[tap : tap + 1] * seen
                            sums[o] = term if sums[o] is None else sums[o] + term
            for o in range(rows):
                conv[t, o, :, :, cols] = sums[o].reshape(groups, SUB, 128)
        return carry

    lax.fori_loop(0, width // 128, conv_step, 0)

    for c in mine + own:
        c.wait()
    for d in col_order:
        for t in range(4):
            p = lax.rem(mc + d, C)
            row_back(t, p, p).wait_recv()
    for ch in range(CHUNKS):
        for d in order:
            for t in range(4):
                p = lax.rem(me + d, R)
                col_back(t, ch, p, p).wait_recv()
    final_copies = [pltpu.make_async_copy(ret.at[t], outs_hbm[t], final.at[t]) for t in (1, 2)]
    for c in final_copies:
        c.start()

    def add_step(n, carry):
        cols = lanes(n * 128, 128)
        for t, source in ((0, 0), (1, 3)):
            done[t, :, :, :, cols] = (ret[source, :, :, :, cols].astype(f32) + conv[t, :, :, :, cols]).astype(jnp.bfloat16)
        return carry

    lax.fori_loop(0, width // 128, add_step, 0)
    last = [pltpu.make_async_copy(done.at[t], outs_hbm[(0, 3)[t]], final.at[(0, 3)[t]]) for t in range(2)]
    for c in last:
        c.start()
    for d in col_order:
        for t in range(4):
            p = lax.rem(mc + d, C)
            row_in(t, p, p).wait_send()
            row_back(t, p, p).wait_send()
    for ch in range(CHUNKS):
        for d in order:
            for t in range(4):
                p = lax.rem(me + d, R)
                col_in(t, ch, p, p).wait_send()
                col_back(t, ch, p, p).wait_send()
    for t in range(2):
        for i in range(8):
            @pl.when(has(i, 1))
            def _(t=t, i=i):
                halo(t, i).wait_send()
    for c in final_copies + last:
        c.wait()


def fused_body(query, key, value, cotangent, conv_weight, row_mask, col_mask):
    rows, cols_here, width = query.shape
    R, C = lax.axis_size("rows"), lax.axis_size("cols")
    groups = cols_here // SUB
    half = width // 2
    share = half // C
    length = R * rows * SUB
    views = [x.reshape(rows, groups, SUB, width) for x in (query, key, value, cotangent)]
    row_allow = jnp.repeat(row_mask.astype(jnp.float32), cols_here * C // SHEET_ROW_BLOCKS, axis=2)
    tables = lax.dynamic_slice_in_dim(col_mask, lax.axis_index("rows") * SUB, SUB, 0)
    spread = jnp.repeat(jnp.transpose(tables, (1, 0, 2)).astype(jnp.float32), length // COL_BLOCKS, axis=2)
    same = lax.broadcasted_iota(jnp.int32, (1, SUB, length), 1) == lax.broadcasted_iota(jnp.int32, (1, SUB, length), 2) % SUB
    col_allow = jnp.where(same, spread, 0.0)
    bf16 = jnp.bfloat16
    any_spec = pl.BlockSpec(memory_space=pl.ANY)
    vmem = pl.BlockSpec(memory_space=pltpu.VMEM)
    dma = pltpu.SemaphoreType.DMA
    outs = pl.pallas_call(
        functools.partial(layer_kernel, (R, C, rows, groups, width)),
        out_shape=[jax.ShapeDtypeStruct((rows, groups, SUB, width), bf16)] * 4,
        in_specs=[any_spec] * 4 + [vmem] * 3,
        out_specs=[any_spec] * 4,
        scratch_shapes=[
            pltpu.VMEM((4, R, rows, SUB, half), bf16),
            pltpu.VMEM((4, R, rows, SUB, half), bf16),
            pltpu.VMEM((4, rows, C, groups, SUB, share), bf16),
            pltpu.VMEM((4, rows, C, groups, SUB, share), bf16),
            pltpu.VMEM((2, rows + 2, groups + 2, SUB, width), bf16),
            pltpu.VMEM((2, rows, groups, SUB, width), jnp.float32),
            pltpu.VMEM((4, rows, groups, SUB, width), bf16),
            pltpu.VMEM((2, rows, groups, SUB, width), bf16),
            dma((4, CHUNKS, R)), dma((4, CHUNKS, R)), dma((4, CHUNKS, R)), dma((4, CHUNKS, R)),
            dma((4, C)), dma((4, C)), dma((4, C)), dma((4, C)),
            dma((2, 8)), dma((2, 8)), dma((3, 4)), dma((4,)),
        ],
        compiler_params=pltpu.CompilerParams(collective_id=0, has_side_effects=True, vmem_limit_bytes=56 << 20),
    )(*views, conv_weight, row_allow, col_allow)
    return tuple(x.reshape(query.shape) for x in outs)


def any_body(query, key, value, cotangent, conv_weight, row_mask, col_mask):
    rows, cols_here, width = query.shape
    R, C = lax.axis_size("rows"), lax.axis_size("cols")
    fits = cols_here == R * SUB and (width // 2) % (C * HEAD_DIM) == 0
    chosen = fused_body if fits else body
    return chosen(query, key, value, cotangent, conv_weight, row_mask, col_mask)


def solution(mesh):
    return jax.shard_map(
        any_body,
        mesh=mesh,
        in_specs=(
            P("rows", "cols", None),
            P("rows", "cols", None),
            P("rows", "cols", None),
            P("rows", "cols", None),
            P(),
            P("rows", None, None),
            P("cols", None, None),
        ),
        out_specs=(
            P("rows", "cols", None),
            P("rows", "cols", None),
            P("rows", "cols", None),
            P("rows", "cols", None),
        ),
        check_vma=False,
    )
```

```python
import functools
import math

import jax
import jax.numpy as jnp
from jax import lax
from jax.experimental import pallas as pl
from jax.experimental.pallas import tpu as pltpu
from jax.sharding import PartitionSpec as P

HEAD_DIM = 128
SHEET_ROW_BLOCKS = 2
COL_BLOCKS = 3


def padded(array, sides, width):
    for axis, dim in sides:
        devices, length = (lax.axis_size(axis), array.shape[dim])
        up = [(i, (i + 1) % devices) for i in range(devices - 1)]
        down = [(j, i) for i, j in up]
        last = lax.slice_in_dim(array, length - width, length, axis=dim)
        leading = lax.slice_in_dim(array, 0, width, axis=dim)
        before = lax.ppermute(last, axis, up)
        after = lax.ppermute(leading, axis, down)
        array = jnp.concatenate([before, array, after], axis=dim)
    return array


def block_allow(block_mask_table, query_pos, key_pos, block_len, block_count):
    labels = jnp.arange(block_count)
    query_onehot_rows = (query_pos[:, None] // block_len == labels[None, :]).astype(jnp.float32)
    key_onehot_rows = (key_pos[:, None] // block_len == labels[None, :]).astype(jnp.float32)
    merged_links = jnp.einsum(
        "xv,zvs,hs->zxh", query_onehot_rows, block_mask_table.astype(jnp.float32), key_onehot_rows
    )
    return merged_links > 0.5


def line_attention(query_part, key_part, value_part, grad_part, allowed, layout):
    if layout == "bq":
        query_form = "bqhd"
        key_layout_shape = "bkhd"
    else:
        query_form = "qbhd"
        key_layout_shape = "kbhd"
    score_scale = 1.0 / math.sqrt(query_part.shape[-1])
    pair_form = query_form + "," + key_layout_shape + "->bhqk"
    scores = (
        jnp.einsum(pair_form, query_part, key_part, preferred_element_type=jnp.float32)
        * score_scale
    )
    scores = jnp.where(allowed[:, None], scores, -jnp.inf)
    highest = jnp.max(scores, axis=-1, keepdims=True)
    weights = jnp.exp(scores - highest)
    weights = weights / jnp.sum(weights, axis=-1, keepdims=True)
    rounded = weights.astype(jnp.bfloat16)
    attended = jnp.einsum(
        "bhqk," + key_layout_shape + "->" + query_form,
        rounded,
        value_part,
        preferred_element_type=jnp.float32,
    )
    dweights = jnp.einsum(pair_form, grad_part, value_part, preferred_element_type=jnp.float32)
    delta = jnp.sum(grad_part.astype(jnp.float32) * attended, axis=-1)
    if layout == "bq":
        delta = jnp.transpose(delta, (0, 2, 1))
    else:
        delta = jnp.transpose(delta, (1, 2, 0))
    dscores = (weights * (dweights - delta[..., None]) * score_scale).astype(jnp.bfloat16)
    dquery = jnp.einsum(
        "bhqk," + key_layout_shape + "->" + query_form,
        dscores,
        key_part,
        preferred_element_type=jnp.float32,
    )
    dkey = jnp.einsum(
        "bhqk," + query_form + "->" + key_layout_shape,
        dscores,
        query_part,
        preferred_element_type=jnp.float32,
    )
    dvalue = jnp.einsum(
        "bhqk," + query_form + "->" + key_layout_shape,
        rounded,
        grad_part,
        preferred_element_type=jnp.float32,
    )
    return (attended, dquery, dkey, dvalue)


def depthwise(padded_field, taps, rows_count, cols_count, reverse_taps):
    summed = jnp.zeros((rows_count, cols_count, taps.shape[1]), jnp.float32)
    for row_offset_start in range(3):
        for offset_col in range(3):
            if reverse_taps:
                start_row = 2 - row_offset_start
                start_col = 2 - offset_col
            else:
                start_row = row_offset_start
                start_col = offset_col
            window = padded_field[
                start_row : start_row + rows_count, start_col : start_col + cols_count
            ]
            summed = summed + taps[row_offset_start * 3 + offset_col] * window.astype(jnp.float32)
    return summed


def body(query, key, value, cotangent, conv_weight, row_mask, col_mask):
    rows_here, cols_here, width = query.shape
    half_width = width // 2
    head_groups = half_width // HEAD_DIM
    row_devices = lax.axis_size("rows")
    col_devices = lax.axis_size("cols")
    sheet_rows = rows_here * row_devices
    sheet_cols = cols_here * col_devices
    taps = conv_weight.astype(jnp.float32)
    padded_value = padded(value, (("rows", 0), ("cols", 1)), 1)
    padded_grad = padded(cotangent, (("rows", 0), ("cols", 1)), 1)
    row_len = sheet_cols // SHEET_ROW_BLOCKS
    keys_row, values_row = (
        lax.all_gather(key[:, :, :half_width], "cols", axis=1, tiled=True),
        lax.all_gather(value[:, :, :half_width], "cols", axis=1, tiled=True),
    )
    col_start = lax.axis_index("cols") * cols_here
    allowed = block_allow(
        row_mask,
        col_start + jnp.arange(cols_here),
        jnp.arange(sheet_cols),
        row_len,
        SHEET_ROW_BLOCKS,
    )
    local_shape = (rows_here, cols_here, head_groups, HEAD_DIM)
    whole_shape = (rows_here, sheet_cols, head_groups, HEAD_DIM)
    results = line_attention(
        query[:, :, :half_width].reshape(local_shape),
        keys_row.reshape(whole_shape),
        values_row.reshape(whole_shape),
        cotangent[:, :, :half_width].reshape(local_shape),
        allowed,
        "bq",
    )
    key_terms = results[2].reshape(rows_here, sheet_cols, half_width)
    value_terms = results[3].reshape(rows_here, sheet_cols, half_width)
    key_grads, value_grads = (
        lax.psum_scatter(key_terms, "cols", scatter_dimension=1, tiled=True),
        lax.psum_scatter(value_terms, "cols", scatter_dimension=1, tiled=True),
    )
    out_row = results[0].reshape(rows_here, cols_here, half_width).astype(jnp.bfloat16)
    dq_row = results[1].reshape(rows_here, cols_here, half_width).astype(jnp.bfloat16)
    dk_row = key_grads.astype(jnp.bfloat16)
    dv_row = value_grads.astype(jnp.bfloat16)
    columns_each = cols_here // row_devices
    moved = (
        lax.all_to_all(query[:, :, half_width:], "rows", split_axis=1, concat_axis=0, tiled=True),
        lax.all_to_all(key[:, :, half_width:], "rows", split_axis=1, concat_axis=0, tiled=True),
        lax.all_to_all(value[:, :, half_width:], "rows", split_axis=1, concat_axis=0, tiled=True),
        lax.all_to_all(
            cotangent[:, :, half_width:], "rows", split_axis=1, concat_axis=0, tiled=True
        ),
    )
    column_shape = (sheet_rows, columns_each, head_groups, HEAD_DIM)
    my_tables = lax.dynamic_slice_in_dim(
        col_mask, lax.axis_index("rows") * columns_each, columns_each, 0
    )
    col_len = sheet_rows // COL_BLOCKS
    positions = jnp.arange(sheet_rows)
    col_allowed = block_allow(my_tables, positions, positions, col_len, COL_BLOCKS)
    col_results = line_attention(
        moved[0].reshape(column_shape),
        moved[1].reshape(column_shape),
        moved[2].reshape(column_shape),
        moved[3].reshape(column_shape),
        col_allowed,
        "qb",
    )
    column_flat = (sheet_rows, columns_each, half_width)
    col_pieces = [piece.reshape(column_flat).astype(jnp.bfloat16) for piece in col_results]
    out_col, dq_col, dk_col, dv_col = (
        lax.all_to_all(col_pieces[0], "rows", split_axis=0, concat_axis=1, tiled=True),
        lax.all_to_all(col_pieces[1], "rows", split_axis=0, concat_axis=1, tiled=True),
        lax.all_to_all(col_pieces[2], "rows", split_axis=0, concat_axis=1, tiled=True),
        lax.all_to_all(col_pieces[3], "rows", split_axis=0, concat_axis=1, tiled=True),
    )
    lepe = depthwise(padded_value, taps, rows_here, cols_here, False)
    back_conv = depthwise(padded_grad, taps, rows_here, cols_here, True)
    attended16 = jnp.concatenate([out_row, out_col], axis=2)
    out = (attended16.astype(jnp.float32) + lepe).astype(jnp.bfloat16)
    dquery = jnp.concatenate([dq_row, dq_col], axis=2)
    dkey = jnp.concatenate([dk_row, dk_col], axis=2)
    dvalue_attn = jnp.concatenate([dv_row, dv_col], axis=2)
    dvalue = (dvalue_attn.astype(jnp.float32) + back_conv).astype(jnp.bfloat16)
    return (out, dquery, dkey, dvalue)


SUB = 8
CHUNKS = 2
MESH = pl.DeviceIdType.MESH


def attend(q, k, v, g, allow):
    scale = 1.0 / math.sqrt(HEAD_DIM)
    nt = (((1,), (1,)), ((), ()))
    nn = (((1,), (0,)), ((), ()))
    tn = (((0,), (0,)), ((), ()))
    dot = functools.partial(lax.dot_general, preferred_element_type=jnp.float32)
    s = jnp.where(allow, dot(q, k, nt) * scale, -jnp.inf)
    e = jnp.exp(s - jnp.max(s, axis=-1, keepdims=True))
    w = e * (1.0 / jnp.sum(e, axis=-1, keepdims=True))
    w16 = w.astype(jnp.bfloat16)
    att = dot(w16, v, nn)
    dw = dot(g, v, nt)
    delta = jnp.sum(g.astype(jnp.float32) * att, axis=-1, keepdims=True)
    ds = (w * (dw - delta) * scale).astype(jnp.bfloat16)
    return att, dot(ds, k, nn), dot(ds, q, tn), dot(w16, g, tn)


def layer_kernel(
    dims, q_hbm, k_hbm, v_hbm, g_hbm, taps, row_mask, col_mask, ret, conv_hbm, *rest
):
    R, C, rows, groups, width = dims
    colbuf, colout, rowbuf, rowout, ext, conv, hop = rest[:7]
    (ci_s, ci_r, co_s, co_r, ri_s, ri_r, ro_s, ro_r, ha_s, ha_r, local) = rest[7:]
    half = width // 2
    share = half // C
    part = half // CHUNKS
    me = lax.axis_index("rows")
    mc = lax.axis_index("cols")
    inputs = (q_hbm, k_hbm, v_hbm, g_hbm)
    f32 = jnp.float32

    def lanes(start, size):
        return pl.ds(pl.multiple_of(start, 128), size)

    def col_in(t, ch, p, slot):
        return pltpu.make_async_remote_copy(
            src_ref=inputs[t].at[:, p, :, pl.ds(half + ch * part, part)],
            dst_ref=colbuf.at[t, slot, :, :, pl.ds(ch * part, part)],
            send_sem=ci_s.at[t, ch, p], recv_sem=ci_r.at[t, ch, slot],
            device_id={"rows": p}, device_id_type=MESH)

    def col_back(t, ch, p, slot):
        return pltpu.make_async_remote_copy(
            src_ref=colout.at[t, p, :, :, pl.ds(ch * part, part)],
            dst_ref=ret.at[t, :, slot, :, pl.ds(half + ch * part, part)],
            send_sem=co_s.at[t, ch, p], recv_sem=co_r.at[t, ch, slot],
            device_id={"rows": p}, device_id_type=MESH)

    def row_in(t, p, slot):
        return pltpu.make_async_remote_copy(
            src_ref=inputs[t].at[:, :, :, lanes(p * share, share)],
            dst_ref=rowbuf.at[t, :, slot],
            send_sem=ri_s.at[t, p], recv_sem=ri_r.at[t, slot],
            device_id={"cols": p}, device_id_type=MESH)

    def row_back(t, p, slot):
        return pltpu.make_async_remote_copy(
            src_ref=rowout.at[t, :, p],
            dst_ref=ret.at[t, :, :, :, lanes(slot * share, share)],
            send_sem=ro_s.at[t, p], recv_sem=ro_r.at[t, slot],
            device_id={"cols": p}, device_id_type=MESH)

    odd = lax.rem(me, 2)
    sign = 2 * odd - 1
    crosses = jnp.logical_and(me + sign >= 0, me + sign < R)
    relays = jnp.logical_and(me - 2 * sign >= 0, me - 2 * sign < R)
    inner = pl.ds(1, groups)

    def halo(kind, t, src, dst, target):
        return pltpu.make_async_remote_copy(
            src_ref=src, dst_ref=dst, send_sem=ha_s.at[kind, t], recv_sem=ha_r.at[kind, t],
            device_id=target, device_id_type=MESH)

    def cross(t, slot):
        return halo(0, t, inputs[2 + t].at[odd * (rows - 1), :, :, pl.ds(0, half)],
                    ext.at[t, slot, inner, :, pl.ds(0, half)], {"rows": me + sign})

    def detour(t):
        return halo(1, t, inputs[2 + t].at[odd * (rows - 1), :, :, pl.ds(half, half)],
                    hop.at[t], {"rows": me + 2 * sign})

    def forward(t, slot):
        return halo(2, t, hop.at[t], ext.at[t, slot, inner, :, pl.ds(half, half)], {"rows": me - sign})

    def near(t, slot):
        return halo(3, t, inputs[2 + t].at[(1 - odd) * (rows - 1)], ext.at[t, slot, inner], {"rows": me - sign})

    def rightward(t):
        return halo(4, t, ext.at[t, :, groups], ext.at[t, :, 0], {"cols": mc + 1})

    def leftward(t):
        return halo(5, t, ext.at[t, :, 1], ext.at[t, :, groups + 1], {"cols": mc - 1})

    even_slot, odd_slot = (1 - odd) * (rows + 1), odd * (rows + 1)

    barrier = pltpu.get_barrier_semaphore()
    for d in range(1, R):
        pl.semaphore_signal(barrier, inc=1, device_id={"rows": lax.rem(me + d, R)}, device_id_type=MESH)
    for d in range(1, C):
        pl.semaphore_signal(barrier, inc=1, device_id={"cols": lax.rem(mc + d, C)}, device_id_type=MESH)
    pl.semaphore_wait(barrier, R - 1 + C - 1)

    order = sorted(range(1, R), key=lambda d: abs(d - R / 2))
    col_order = sorted(range(1, C), key=lambda d: abs(d - C / 2))
    for d in col_order:
        for t in range(4):
            row_in(t, lax.rem(mc + d, C), mc).start()
    for ch in range(CHUNKS):
        for d in order:
            for t in range(4):
                col_in(t, ch, lax.rem(me + d, R), me).start()
    @pl.when(crosses)
    def _():
        for t in range(2):
            detour(t).start()
            cross(t, even_slot).start()
    for t in range(2):
        near(t, odd_slot).start()

    mine = []
    for t in range(4):
        mine.append(pltpu.make_async_copy(inputs[t].at[:, :, :, lanes(mc * share, share)], rowbuf.at[t, :, mc], local.at[0, t]))
        mine.append(pltpu.make_async_copy(inputs[t].at[:, me, :, pl.ds(half, half)], colbuf.at[t, me], local.at[1, t]))
    for t in range(2):
        mine.append(pltpu.make_async_copy(inputs[2 + t], ext.at[t, pl.ds(1, rows), pl.ds(1, groups)], local.at[2, t]))
    for c in mine:
        c.start()
    for edge, area in (
        (me == 0, (slice(None), 0, inner)),
        (me == R - 1, (slice(None), rows + 1, inner)),
        (mc == 0, (slice(None), slice(None), 0)),
        (mc == C - 1, (slice(None), slice(None), groups + 1)),
    ):
        @pl.when(edge)
        def _(area=area):
            view = ext.at[area]
            view[...] = jnp.zeros(view.shape, view.dtype)
    for c in mine:
        c.wait()

    length = R * rows * SUB
    col_size = length // COL_BLOCKS
    key_pos = lax.broadcasted_iota(jnp.int32, (SUB, length), 1)
    lane_col = lax.broadcasted_iota(jnp.int32, (SUB, length), 0)
    block = jnp.where(lax.rem(key_pos, SUB) == lane_col, key_pos // col_size, -1)
    col_tables = []
    for b in range(COL_BLOCKS):
        table = jnp.zeros((SUB, length), jnp.int32)
        for c in range(SUB):
            for j in range(COL_BLOCKS):
                here = jnp.logical_and(lane_col == c, block == j)
                table = jnp.where(here, col_mask[me * SUB + c, b, j], table)
        col_tables.append(table)

    for d in col_order:
        for t in range(4):
            p = lax.rem(mc + d, C)
            row_in(t, p, p).wait_recv()
    tokens = C * groups * SUB

    def row_step(n, carry):
        i, h = n // (share // HEAD_DIM), lax.rem(n, share // HEAD_DIM)
        cols = lanes(h * HEAD_DIM, HEAD_DIM)
        x = [rowbuf[t, i, :, :, :, cols].astype(f32).reshape(tokens, HEAD_DIM).astype(jnp.bfloat16) for t in range(4)]
        size = tokens // SHEET_ROW_BLOCKS
        place = lax.broadcasted_iota(jnp.int32, (SUB, tokens), 1) // size
        bands = []
        for b in range(SHEET_ROW_BLOCKS):
            table = jnp.zeros((SUB, tokens), jnp.int32)
            for j in range(SHEET_ROW_BLOCKS):
                table = jnp.where(place == j, row_mask[i, b, j], table)
            bands.append(jnp.broadcast_to(table[None], (size // SUB, SUB, tokens)).reshape(size, tokens))
        allow = jnp.concatenate(bands, axis=0) > 0
        for t, y in enumerate(attend(*x, allow)):
            rowout[t, i, :, :, :, cols] = y.reshape(C, groups, SUB, HEAD_DIM).astype(jnp.bfloat16)
        return carry

    lax.fori_loop(0, rows * (share // HEAD_DIM), row_step, 0)
    for d in col_order:
        for t in range(4):
            row_back(t, lax.rem(mc + d, C), mc).start()
    mine = [pltpu.make_async_copy(rowout.at[t, :, mc], ret.at[t, :, :, :, lanes(mc * share, share)], local.at[0, t]) for t in range(4)]
    for c in mine:
        c.start()

    for ch in range(CHUNKS):
        for d in order:
            for t in range(4):
                p = lax.rem(me + d, R)
                col_in(t, ch, p, p).wait_recv()
        allow = jnp.concatenate(
            [jnp.broadcast_to(t[None], (col_size // SUB, SUB, length)).reshape(col_size, length) for t in col_tables], axis=0) > 0

        def col_step(h, carry):
            cols = lanes(ch * part + h * HEAD_DIM, HEAD_DIM)
            x = [colbuf[t, :, :, :, cols].astype(f32).reshape(length, HEAD_DIM).astype(jnp.bfloat16) for t in range(4)]
            for t, y in enumerate(attend(*x, allow)):
                colout[t, :, :, :, cols] = y.reshape(R, rows, SUB, HEAD_DIM).astype(jnp.bfloat16)
            return carry

        lax.fori_loop(0, part // HEAD_DIM, col_step, 0)
        for d in order:
            for t in range(4):
                col_back(t, ch, lax.rem(me + d, R), me).start()
    own = [pltpu.make_async_copy(colout.at[t, me], ret.at[t, :, me, :, pl.ds(half, half)], local.at[1, t]) for t in range(4)]
    for c in own:
        c.start()

    @pl.when(relays)
    def _():
        for t in range(2):
            detour(t).wait_recv()
            forward(t, even_slot).start()
    for t in range(2):
        near(t, even_slot).wait_recv()

    @pl.when(crosses)
    def _():
        for t in range(2):
            cross(t, odd_slot).wait_recv()
            forward(t, odd_slot).wait_recv()

    @pl.when(mc < C - 1)
    def _():
        for t in range(2):
            rightward(t).start()

    @pl.when(mc > 0)
    def _():
        for t in range(2):
            leftward(t).start()

    @pl.when(mc > 0)
    def _():
        for t in range(2):
            rightward(t).wait_recv()

    @pl.when(mc < C - 1)
    def _():
        for t in range(2):
            leftward(t).wait_recv()
    long = groups * SUB

    def conv_step(n, carry):
        cols = lanes(n * 128, 128)
        weights = taps[:, cols].astype(f32)
        for t in range(2):
            sums = [None] * rows
            for r in range(rows + 2):
                line = ext[t, r, :, :, cols].astype(f32).reshape(long + 2 * SUB, 128)
                for b in range(3):
                    seen = line[SUB + b - 1 : SUB + b - 1 + long]
                    for a in range(3):
                        o = r - a
                        if 0 <= o < rows:
                            tap = 3 * a + b if t == 0 else 8 - 3 * a - b
                            term = weights[tap : tap + 1] * seen
                            sums[o] = term if sums[o] is None else sums[o] + term
            for o in range(rows):
                conv[t, o, :, :, cols] = sums[o].reshape(groups, SUB, 128)
        return carry

    lax.fori_loop(0, width // 128, conv_step, 0)
    keep = pltpu.make_async_copy(conv, conv_hbm, local.at[2, 2])
    keep.start()

    for c in mine + own:
        c.wait()
    for d in col_order:
        for t in range(4):
            p = lax.rem(mc + d, C)
            row_back(t, p, p).wait_recv()
    for ch in range(CHUNKS):
        for d in order:
            for t in range(4):
                p = lax.rem(me + d, R)
                col_back(t, ch, p, p).wait_recv()
    for d in col_order:
        for t in range(4):
            p = lax.rem(mc + d, C)
            row_in(t, p, p).wait_send()
            row_back(t, p, p).wait_send()
    for ch in range(CHUNKS):
        for d in order:
            for t in range(4):
                p = lax.rem(me + d, R)
                col_in(t, ch, p, p).wait_send()
                col_back(t, ch, p, p).wait_send()
    for t in range(2):
        near(t, odd_slot).wait_send()

    @pl.when(crosses)
    def _():
        for t in range(2):
            cross(t, even_slot).wait_send()
            detour(t).wait_send()

    @pl.when(relays)
    def _():
        for t in range(2):
            forward(t, even_slot).wait_send()

    @pl.when(mc < C - 1)
    def _():
        for t in range(2):
            rightward(t).wait_send()

    @pl.when(mc > 0)
    def _():
        for t in range(2):
            leftward(t).wait_send()
    keep.wait()


def finish_kernel(ret, conv, out, dquery, dkey, dvalue):
    out[...] = (ret[0].astype(jnp.float32) + conv[0]).astype(jnp.bfloat16)
    dquery[...] = ret[1]
    dkey[...] = ret[2]
    dvalue[...] = (ret[3].astype(jnp.float32) + conv[1]).astype(jnp.bfloat16)


def fused_body(query, key, value, cotangent, conv_weight, row_mask, col_mask):
    rows, cols_here, width = query.shape
    R, C = lax.axis_size("rows"), lax.axis_size("cols")
    groups = cols_here // SUB
    half = width // 2
    share = half // C
    views = [x.reshape(rows, groups, SUB, width) for x in (query, key, value, cotangent)]
    bf16 = jnp.bfloat16
    any_spec = pl.BlockSpec(memory_space=pl.ANY)
    vmem = pl.BlockSpec(memory_space=pltpu.VMEM)
    dma = pltpu.SemaphoreType.DMA
    smem = pl.BlockSpec(memory_space=pltpu.SMEM)
    ret, conv = pl.pallas_call(
        functools.partial(layer_kernel, (R, C, rows, groups, width)),
        out_shape=[jax.ShapeDtypeStruct((4, rows, groups, SUB, width), bf16), jax.ShapeDtypeStruct((2, rows, groups, SUB, width), jnp.float32)],
        in_specs=[any_spec] * 4 + [vmem, smem, smem],
        out_specs=[any_spec] * 2,
        scratch_shapes=[
            pltpu.VMEM((4, R, rows, SUB, half), bf16),
            pltpu.VMEM((4, R, rows, SUB, half), bf16),
            pltpu.VMEM((4, rows, C, groups, SUB, share), bf16),
            pltpu.VMEM((4, rows, C, groups, SUB, share), bf16),
            pltpu.VMEM((2, rows + 2, groups + 2, SUB, width), bf16),
            pltpu.VMEM((2, rows, groups, SUB, width), jnp.float32),
            pltpu.VMEM((2, groups, SUB, half), bf16),
            dma((4, CHUNKS, R)), dma((4, CHUNKS, R)), dma((4, CHUNKS, R)), dma((4, CHUNKS, R)),
            dma((4, C)), dma((4, C)), dma((4, C)), dma((4, C)),
            dma((6, 2)), dma((6, 2)), dma((3, 4)),
        ],
        compiler_params=pltpu.CompilerParams(collective_id=0, has_side_effects=True, vmem_limit_bytes=56 << 20),
    )(*views, conv_weight, row_mask, col_mask)
    split = 2
    one = pl.BlockSpec((1, groups, SUB, width // split), lambda i, j: (i, 0, 0, j))
    outs = pl.pallas_call(
        finish_kernel,
        out_shape=[jax.ShapeDtypeStruct((rows, groups, SUB, width), bf16)] * 4,
        grid=(rows, split),
        in_specs=[
            pl.BlockSpec((4, 1, groups, SUB, width // split), lambda i, j: (0, i, 0, 0, j)),
            pl.BlockSpec((2, 1, groups, SUB, width // split), lambda i, j: (0, i, 0, 0, j)),
        ],
        out_specs=[one] * 4,
    )(ret, conv)
    return tuple(x.reshape(query.shape) for x in outs)


def any_body(query, key, value, cotangent, conv_weight, row_mask, col_mask):
    rows, cols_here, width = query.shape
    R, C = lax.axis_size("rows"), lax.axis_size("cols")
    fits = R % 2 == 0 and cols_here == R * SUB and (width // 2) % (C * HEAD_DIM) == 0
    chosen = fused_body if fits else body
    return chosen(query, key, value, cotangent, conv_weight, row_mask, col_mask)


def solution(mesh):
    return jax.shard_map(
        any_body,
        mesh=mesh,
        in_specs=(
            P("rows", "cols", None),
            P("rows", "cols", None),
            P("rows", "cols", None),
            P("rows", "cols", None),
            P(),
            P("rows", None, None),
            P("cols", None, None),
        ),
        out_specs=(
            P("rows", "cols", None),
            P("rows", "cols", None),
            P("rows", "cols", None),
            P("rows", "cols", None),
        ),
        check_vma=False,
    )
```

```python
import functools
import math

import jax
import jax.numpy as jnp
from jax import lax
from jax.experimental import pallas as pl
from jax.experimental.pallas import tpu as pltpu
from jax.sharding import PartitionSpec as P

HEAD_DIM = 128
SHEET_ROW_BLOCKS = 2
COL_BLOCKS = 3


def padded(array, sides, width):
    for axis, dim in sides:
        devices, length = (lax.axis_size(axis), array.shape[dim])
        up = [(i, (i + 1) % devices) for i in range(devices - 1)]
        down = [(j, i) for i, j in up]
        last = lax.slice_in_dim(array, length - width, length, axis=dim)
        leading = lax.slice_in_dim(array, 0, width, axis=dim)
        before = lax.ppermute(last, axis, up)
        after = lax.ppermute(leading, axis, down)
        array = jnp.concatenate([before, array, after], axis=dim)
    return array


def block_allow(block_mask_table, query_pos, key_pos, block_len, block_count):
    labels = jnp.arange(block_count)
    query_onehot_rows = (query_pos[:, None] // block_len == labels[None, :]).astype(jnp.float32)
    key_onehot_rows = (key_pos[:, None] // block_len == labels[None, :]).astype(jnp.float32)
    merged_links = jnp.einsum(
        "xv,zvs,hs->zxh", query_onehot_rows, block_mask_table.astype(jnp.float32), key_onehot_rows
    )
    return merged_links > 0.5


def line_attention(query_part, key_part, value_part, grad_part, allowed, layout):
    if layout == "bq":
        query_form = "bqhd"
        key_layout_shape = "bkhd"
    else:
        query_form = "qbhd"
        key_layout_shape = "kbhd"
    score_scale = 1.0 / math.sqrt(query_part.shape[-1])
    pair_form = query_form + "," + key_layout_shape + "->bhqk"
    scores = (
        jnp.einsum(pair_form, query_part, key_part, preferred_element_type=jnp.float32)
        * score_scale
    )
    scores = jnp.where(allowed[:, None], scores, -jnp.inf)
    highest = jnp.max(scores, axis=-1, keepdims=True)
    weights = jnp.exp(scores - highest)
    weights = weights / jnp.sum(weights, axis=-1, keepdims=True)
    rounded = weights.astype(jnp.bfloat16)
    attended = jnp.einsum(
        "bhqk," + key_layout_shape + "->" + query_form,
        rounded,
        value_part,
        preferred_element_type=jnp.float32,
    )
    dweights = jnp.einsum(pair_form, grad_part, value_part, preferred_element_type=jnp.float32)
    delta = jnp.sum(grad_part.astype(jnp.float32) * attended, axis=-1)
    if layout == "bq":
        delta = jnp.transpose(delta, (0, 2, 1))
    else:
        delta = jnp.transpose(delta, (1, 2, 0))
    dscores = (weights * (dweights - delta[..., None]) * score_scale).astype(jnp.bfloat16)
    dquery = jnp.einsum(
        "bhqk," + key_layout_shape + "->" + query_form,
        dscores,
        key_part,
        preferred_element_type=jnp.float32,
    )
    dkey = jnp.einsum(
        "bhqk," + query_form + "->" + key_layout_shape,
        dscores,
        query_part,
        preferred_element_type=jnp.float32,
    )
    dvalue = jnp.einsum(
        "bhqk," + query_form + "->" + key_layout_shape,
        rounded,
        grad_part,
        preferred_element_type=jnp.float32,
    )
    return (attended, dquery, dkey, dvalue)


def depthwise(padded_field, taps, rows_count, cols_count, reverse_taps):
    summed = jnp.zeros((rows_count, cols_count, taps.shape[1]), jnp.float32)
    for row_offset_start in range(3):
        for offset_col in range(3):
            if reverse_taps:
                start_row = 2 - row_offset_start
                start_col = 2 - offset_col
            else:
                start_row = row_offset_start
                start_col = offset_col
            window = padded_field[
                start_row : start_row + rows_count, start_col : start_col + cols_count
            ]
            summed = summed + taps[row_offset_start * 3 + offset_col] * window.astype(jnp.float32)
    return summed


def body(query, key, value, cotangent, conv_weight, row_mask, col_mask):
    rows_here, cols_here, width = query.shape
    half_width = width // 2
    head_groups = half_width // HEAD_DIM
    row_devices = lax.axis_size("rows")
    col_devices = lax.axis_size("cols")
    sheet_rows = rows_here * row_devices
    sheet_cols = cols_here * col_devices
    taps = conv_weight.astype(jnp.float32)
    padded_value = padded(value, (("rows", 0), ("cols", 1)), 1)
    padded_grad = padded(cotangent, (("rows", 0), ("cols", 1)), 1)
    row_len = sheet_cols // SHEET_ROW_BLOCKS
    keys_row, values_row = (
        lax.all_gather(key[:, :, :half_width], "cols", axis=1, tiled=True),
        lax.all_gather(value[:, :, :half_width], "cols", axis=1, tiled=True),
    )
    col_start = lax.axis_index("cols") * cols_here
    allowed = block_allow(
        row_mask,
        col_start + jnp.arange(cols_here),
        jnp.arange(sheet_cols),
        row_len,
        SHEET_ROW_BLOCKS,
    )
    local_shape = (rows_here, cols_here, head_groups, HEAD_DIM)
    whole_shape = (rows_here, sheet_cols, head_groups, HEAD_DIM)
    results = line_attention(
        query[:, :, :half_width].reshape(local_shape),
        keys_row.reshape(whole_shape),
        values_row.reshape(whole_shape),
        cotangent[:, :, :half_width].reshape(local_shape),
        allowed,
        "bq",
    )
    key_terms = results[2].reshape(rows_here, sheet_cols, half_width)
    value_terms = results[3].reshape(rows_here, sheet_cols, half_width)
    key_grads, value_grads = (
        lax.psum_scatter(key_terms, "cols", scatter_dimension=1, tiled=True),
        lax.psum_scatter(value_terms, "cols", scatter_dimension=1, tiled=True),
    )
    out_row = results[0].reshape(rows_here, cols_here, half_width).astype(jnp.bfloat16)
    dq_row = results[1].reshape(rows_here, cols_here, half_width).astype(jnp.bfloat16)
    dk_row = key_grads.astype(jnp.bfloat16)
    dv_row = value_grads.astype(jnp.bfloat16)
    columns_each = cols_here // row_devices
    moved = (
        lax.all_to_all(query[:, :, half_width:], "rows", split_axis=1, concat_axis=0, tiled=True),
        lax.all_to_all(key[:, :, half_width:], "rows", split_axis=1, concat_axis=0, tiled=True),
        lax.all_to_all(value[:, :, half_width:], "rows", split_axis=1, concat_axis=0, tiled=True),
        lax.all_to_all(
            cotangent[:, :, half_width:], "rows", split_axis=1, concat_axis=0, tiled=True
        ),
    )
    column_shape = (sheet_rows, columns_each, head_groups, HEAD_DIM)
    my_tables = lax.dynamic_slice_in_dim(
        col_mask, lax.axis_index("rows") * columns_each, columns_each, 0
    )
    col_len = sheet_rows // COL_BLOCKS
    positions = jnp.arange(sheet_rows)
    col_allowed = block_allow(my_tables, positions, positions, col_len, COL_BLOCKS)
    col_results = line_attention(
        moved[0].reshape(column_shape),
        moved[1].reshape(column_shape),
        moved[2].reshape(column_shape),
        moved[3].reshape(column_shape),
        col_allowed,
        "qb",
    )
    column_flat = (sheet_rows, columns_each, half_width)
    col_pieces = [piece.reshape(column_flat).astype(jnp.bfloat16) for piece in col_results]
    out_col, dq_col, dk_col, dv_col = (
        lax.all_to_all(col_pieces[0], "rows", split_axis=0, concat_axis=1, tiled=True),
        lax.all_to_all(col_pieces[1], "rows", split_axis=0, concat_axis=1, tiled=True),
        lax.all_to_all(col_pieces[2], "rows", split_axis=0, concat_axis=1, tiled=True),
        lax.all_to_all(col_pieces[3], "rows", split_axis=0, concat_axis=1, tiled=True),
    )
    lepe = depthwise(padded_value, taps, rows_here, cols_here, False)
    back_conv = depthwise(padded_grad, taps, rows_here, cols_here, True)
    attended16 = jnp.concatenate([out_row, out_col], axis=2)
    out = (attended16.astype(jnp.float32) + lepe).astype(jnp.bfloat16)
    dquery = jnp.concatenate([dq_row, dq_col], axis=2)
    dkey = jnp.concatenate([dk_row, dk_col], axis=2)
    dvalue_attn = jnp.concatenate([dv_row, dv_col], axis=2)
    dvalue = (dvalue_attn.astype(jnp.float32) + back_conv).astype(jnp.bfloat16)
    return (out, dquery, dkey, dvalue)


SUB = 8
CHUNKS = 1
MESH = pl.DeviceIdType.MESH


def attend(q, k, v, g, allow):
    scale = 1.0 / math.sqrt(HEAD_DIM)
    nt = (((1,), (1,)), ((), ()))
    nn = (((1,), (0,)), ((), ()))
    tn = (((0,), (0,)), ((), ()))
    dot = functools.partial(lax.dot_general, preferred_element_type=jnp.float32)
    s = jnp.where(allow, dot(q, k, nt) * scale, -jnp.inf)
    e = jnp.exp(s - jnp.max(s, axis=-1, keepdims=True))
    w = e * (1.0 / jnp.sum(e, axis=-1, keepdims=True))
    w16 = w.astype(jnp.bfloat16)
    att = dot(w16, v, nn)
    dw = dot(g, v, nt)
    delta = jnp.sum(g.astype(jnp.float32) * att, axis=-1, keepdims=True)
    ds = (w * (dw - delta) * scale).astype(jnp.bfloat16)
    return att, dot(ds, k, nn), dot(ds, q, tn), dot(w16, g, tn)


def layer_kernel(
    dims, q_hbm, k_hbm, v_hbm, g_hbm, taps, row_mask, col_mask, ret, conv_hbm, *rest
):
    R, C, rows, groups, width = dims
    colbuf, colout, rowbuf, rowout, ext, conv, hop = rest[:7]
    (ci_s, ci_r, co_s, co_r, ri_s, ri_r, ro_s, ro_r, ha_s, ha_r, local) = rest[7:]
    half = width // 2
    share = half // C
    part = half // CHUNKS
    me = lax.axis_index("rows")
    mc = lax.axis_index("cols")
    inputs = (q_hbm, k_hbm, v_hbm, g_hbm)
    f32 = jnp.float32

    def lanes(start, size):
        return pl.ds(pl.multiple_of(start, 128), size)

    def col_in(t, ch, p, slot):
        return pltpu.make_async_remote_copy(
            src_ref=inputs[t].at[:, p, :, pl.ds(half + ch * part, part)],
            dst_ref=colbuf.at[t, slot, :, :, pl.ds(ch * part, part)],
            send_sem=ci_s.at[t, ch, p], recv_sem=ci_r.at[t, ch, slot],
            device_id={"rows": p}, device_id_type=MESH)

    def col_back(t, ch, p, slot):
        return pltpu.make_async_remote_copy(
            src_ref=colout.at[t, p, :, :, pl.ds(ch * part, part)],
            dst_ref=ret.at[t, :, slot, :, pl.ds(half + ch * part, part)],
            send_sem=co_s.at[t, ch, p], recv_sem=co_r.at[t, ch, slot],
            device_id={"rows": p}, device_id_type=MESH)

    def row_in(t, p, slot):
        return pltpu.make_async_remote_copy(
            src_ref=inputs[t].at[:, :, :, lanes(p * share, share)],
            dst_ref=rowbuf.at[t, :, slot],
            send_sem=ri_s.at[t, p], recv_sem=ri_r.at[t, slot],
            device_id={"cols": p}, device_id_type=MESH)

    def row_back(t, p, slot):
        return pltpu.make_async_remote_copy(
            src_ref=rowout.at[t, :, p],
            dst_ref=ret.at[t, :, :, :, lanes(slot * share, share)],
            send_sem=ro_s.at[t, p], recv_sem=ro_r.at[t, slot],
            device_id={"cols": p}, device_id_type=MESH)

    odd = lax.rem(me, 2)
    sign = 2 * odd - 1
    crosses = jnp.logical_and(me + sign >= 0, me + sign < R)
    relays = jnp.logical_and(me - 2 * sign >= 0, me - 2 * sign < R)
    inner = pl.ds(1, groups)

    def halo(kind, t, src, dst, target):
        return pltpu.make_async_remote_copy(
            src_ref=src, dst_ref=dst, send_sem=ha_s.at[kind, t], recv_sem=ha_r.at[kind, t],
            device_id=target, device_id_type=MESH)

    def cross(t, slot):
        return halo(0, t, inputs[2 + t].at[odd * (rows - 1), :, :, pl.ds(0, half)],
                    ext.at[t, slot, inner, :, pl.ds(0, half)], {"rows": me + sign})

    def detour(t):
        return halo(1, t, inputs[2 + t].at[odd * (rows - 1), :, :, pl.ds(half, half)],
                    hop.at[t], {"rows": me + 2 * sign})

    def forward(t, slot):
        return halo(2, t, hop.at[t], ext.at[t, slot, inner, :, pl.ds(half, half)], {"rows": me - sign})

    def near(t, slot):
        return halo(3, t, inputs[2 + t].at[(1 - odd) * (rows - 1)], ext.at[t, slot, inner], {"rows": me - sign})

    def rightward(t):
        return halo(4, t, ext.at[t, :, groups], ext.at[t, :, 0], {"cols": mc + 1})

    def leftward(t):
        return halo(5, t, ext.at[t, :, 1], ext.at[t, :, groups + 1], {"cols": mc - 1})

    even_slot, odd_slot = (1 - odd) * (rows + 1), odd * (rows + 1)

    barrier = pltpu.get_barrier_semaphore()
    for d in range(1, R):
        pl.semaphore_signal(barrier, inc=1, device_id={"rows": lax.rem(me + d, R)}, device_id_type=MESH)
    for d in range(1, C):
        pl.semaphore_signal(barrier, inc=1, device_id={"cols": lax.rem(mc + d, C)}, device_id_type=MESH)
    pl.semaphore_wait(barrier, R - 1 + C - 1)

    order = sorted(range(1, R), key=lambda d: abs(d - R / 2))
    col_order = sorted(range(1, C), key=lambda d: abs(d - C / 2))
    for d in col_order:
        for t in range(4):
            row_in(t, lax.rem(mc + d, C), mc).start()
    for ch in range(CHUNKS):
        for d in order:
            for t in range(4):
                col_in(t, ch, lax.rem(me + d, R), me).start()
    @pl.when(crosses)
    def _():
        for t in range(2):
            detour(t).start()
            cross(t, even_slot).start()
    for t in range(2):
        near(t, odd_slot).start()

    mine = []
    for t in range(4):
        mine.append(pltpu.make_async_copy(inputs[t].at[:, :, :, lanes(mc * share, share)], rowbuf.at[t, :, mc], local.at[0, t]))
        mine.append(pltpu.make_async_copy(inputs[t].at[:, me, :, pl.ds(half, half)], colbuf.at[t, me], local.at[1, t]))
    for t in range(2):
        mine.append(pltpu.make_async_copy(inputs[2 + t], ext.at[t, pl.ds(1, rows), pl.ds(1, groups)], local.at[2, t]))
    for c in mine:
        c.start()
    for edge, area in (
        (me == 0, (slice(None), 0, inner)),
        (me == R - 1, (slice(None), rows + 1, inner)),
        (mc == 0, (slice(None), slice(None), 0)),
        (mc == C - 1, (slice(None), slice(None), groups + 1)),
    ):
        @pl.when(edge)
        def _(area=area):
            view = ext.at[area]
            view[...] = jnp.zeros(view.shape, view.dtype)
    for c in mine:
        c.wait()

    length = R * rows * SUB
    col_size = length // COL_BLOCKS
    key_pos = lax.broadcasted_iota(jnp.int32, (SUB, length), 1)
    lane_col = lax.broadcasted_iota(jnp.int32, (SUB, length), 0)
    block = jnp.where(lax.rem(key_pos, SUB) == lane_col, key_pos // col_size, -1)
    col_tables = []
    for b in range(COL_BLOCKS):
        table = jnp.zeros((SUB, length), jnp.int32)
        for c in range(SUB):
            for j in range(COL_BLOCKS):
                here = jnp.logical_and(lane_col == c, block == j)
                table = jnp.where(here, col_mask[b, j, me * SUB + c], table)
        col_tables.append(table)

    for d in col_order:
        for t in range(4):
            p = lax.rem(mc + d, C)
            row_in(t, p, p).wait_recv()
    tokens = C * groups * SUB

    def row_step(n, carry):
        i, h = n // (share // HEAD_DIM), lax.rem(n, share // HEAD_DIM)
        cols = lanes(h * HEAD_DIM, HEAD_DIM)
        x = [rowbuf[t, i, :, :, :, cols].astype(f32).reshape(tokens, HEAD_DIM).astype(jnp.bfloat16) for t in range(4)]
        size = tokens // SHEET_ROW_BLOCKS
        place = lax.broadcasted_iota(jnp.int32, (SUB, tokens), 1) // size
        bands = []
        for b in range(SHEET_ROW_BLOCKS):
            table = jnp.zeros((SUB, tokens), jnp.int32)
            for j in range(SHEET_ROW_BLOCKS):
                table = jnp.where(place == j, row_mask[b, j, i], table)
            bands.append(jnp.broadcast_to(table[None], (size // SUB, SUB, tokens)).reshape(size, tokens))
        allow = jnp.concatenate(bands, axis=0) > 0
        for t, y in enumerate(attend(*x, allow)):
            rowout[t, i, :, :, :, cols] = y.reshape(C, groups, SUB, HEAD_DIM).astype(jnp.bfloat16)
        return carry

    lax.fori_loop(0, rows * (share // HEAD_DIM), row_step, 0)
    for d in col_order:
        for t in range(4):
            row_back(t, lax.rem(mc + d, C), mc).start()
    mine = [pltpu.make_async_copy(rowout.at[t, :, mc], ret.at[t, :, :, :, lanes(mc * share, share)], local.at[0, t]) for t in range(4)]
    for c in mine:
        c.start()

    for ch in range(CHUNKS):
        for d in order:
            for t in range(4):
                p = lax.rem(me + d, R)
                col_in(t, ch, p, p).wait_recv()
        allow = jnp.concatenate(
            [jnp.broadcast_to(t[None], (col_size // SUB, SUB, length)).reshape(col_size, length) for t in col_tables], axis=0) > 0

        def col_step(h, carry):
            cols = lanes(ch * part + h * HEAD_DIM, HEAD_DIM)
            x = [colbuf[t, :, :, :, cols].astype(f32).reshape(length, HEAD_DIM).astype(jnp.bfloat16) for t in range(4)]
            for t, y in enumerate(attend(*x, allow)):
                colout[t, :, :, :, cols] = y.reshape(R, rows, SUB, HEAD_DIM).astype(jnp.bfloat16)
            return carry

        lax.fori_loop(0, part // HEAD_DIM, col_step, 0)
        for d in order:
            for t in range(4):
                col_back(t, ch, lax.rem(me + d, R), me).start()
    own = [pltpu.make_async_copy(colout.at[t, me], ret.at[t, :, me, :, pl.ds(half, half)], local.at[1, t]) for t in range(4)]
    for c in own:
        c.start()

    @pl.when(relays)
    def _():
        for t in range(2):
            detour(t).wait_recv()
            forward(t, even_slot).start()
    for t in range(2):
        near(t, even_slot).wait_recv()

    @pl.when(crosses)
    def _():
        for t in range(2):
            cross(t, odd_slot).wait_recv()
            forward(t, odd_slot).wait_recv()

    @pl.when(mc < C - 1)
    def _():
        for t in range(2):
            rightward(t).start()

    @pl.when(mc > 0)
    def _():
        for t in range(2):
            leftward(t).start()

    @pl.when(mc > 0)
    def _():
        for t in range(2):
            rightward(t).wait_recv()

    @pl.when(mc < C - 1)
    def _():
        for t in range(2):
            leftward(t).wait_recv()
    long = groups * SUB

    def conv_step(n, carry):
        cols = lanes(n * 128, 128)
        weights = taps[:, cols].astype(f32)
        for t in range(2):
            sums = [None] * rows
            for r in range(rows + 2):
                line = ext[t, r, :, :, cols].astype(f32).reshape(long + 2 * SUB, 128)
                for b in range(3):
                    seen = line[SUB + b - 1 : SUB + b - 1 + long]
                    for a in range(3):
                        o = r - a
                        if 0 <= o < rows:
                            tap = 3 * a + b if t == 0 else 8 - 3 * a - b
                            term = weights[tap : tap + 1] * seen
                            sums[o] = term if sums[o] is None else sums[o] + term
            for o in range(rows):
                conv[t, o, :, :, cols] = sums[o].reshape(groups, SUB, 128)
        return carry

    lax.fori_loop(0, width // 128, conv_step, 0)
    keep = pltpu.make_async_copy(conv, conv_hbm, local.at[2, 2])
    keep.start()

    for c in mine + own:
        c.wait()
    for d in col_order:
        for t in range(4):
            p = lax.rem(mc + d, C)
            row_back(t, p, p).wait_recv()
    for ch in range(CHUNKS):
        for d in order:
            for t in range(4):
                p = lax.rem(me + d, R)
                col_back(t, ch, p, p).wait_recv()
    for d in col_order:
        for t in range(4):
            p = lax.rem(mc + d, C)
            row_in(t, p, p).wait_send()
            row_back(t, p, p).wait_send()
    for ch in range(CHUNKS):
        for d in order:
            for t in range(4):
                p = lax.rem(me + d, R)
                col_in(t, ch, p, p).wait_send()
                col_back(t, ch, p, p).wait_send()
    for t in range(2):
        near(t, odd_slot).wait_send()

    @pl.when(crosses)
    def _():
        for t in range(2):
            cross(t, even_slot).wait_send()
            detour(t).wait_send()

    @pl.when(relays)
    def _():
        for t in range(2):
            forward(t, even_slot).wait_send()

    @pl.when(mc < C - 1)
    def _():
        for t in range(2):
            rightward(t).wait_send()

    @pl.when(mc > 0)
    def _():
        for t in range(2):
            leftward(t).wait_send()
    keep.wait()


def finish_kernel(ret, conv, out, dquery, dkey, dvalue):
    out[...] = (ret[0].astype(jnp.float32) + conv[0]).astype(jnp.bfloat16)
    dquery[...] = ret[1]
    dkey[...] = ret[2]
    dvalue[...] = (ret[3].astype(jnp.float32) + conv[1]).astype(jnp.bfloat16)


def fused_body(query, key, value, cotangent, conv_weight, row_mask, col_mask):
    rows, cols_here, width = query.shape
    R, C = lax.axis_size("rows"), lax.axis_size("cols")
    groups = cols_here // SUB
    half = width // 2
    share = half // C
    views = [x.reshape(rows, groups, SUB, width) for x in (query, key, value, cotangent)]
    bf16 = jnp.bfloat16
    any_spec = pl.BlockSpec(memory_space=pl.ANY)
    vmem = pl.BlockSpec(memory_space=pltpu.VMEM)
    dma = pltpu.SemaphoreType.DMA
    smem = pl.BlockSpec(memory_space=pltpu.SMEM)
    ret, conv = pl.pallas_call(
        functools.partial(layer_kernel, (R, C, rows, groups, width)),
        out_shape=[jax.ShapeDtypeStruct((4, rows, groups, SUB, width), bf16), jax.ShapeDtypeStruct((2, rows, groups, SUB, width), jnp.float32)],
        in_specs=[any_spec] * 4 + [vmem, smem, smem],
        out_specs=[any_spec] * 2,
        scratch_shapes=[
            pltpu.VMEM((4, R, rows, SUB, half), bf16),
            pltpu.VMEM((4, R, rows, SUB, half), bf16),
            pltpu.VMEM((4, rows, C, groups, SUB, share), bf16),
            pltpu.VMEM((4, rows, C, groups, SUB, share), bf16),
            pltpu.VMEM((2, rows + 2, groups + 2, SUB, width), bf16),
            pltpu.VMEM((2, rows, groups, SUB, width), jnp.float32),
            pltpu.VMEM((2, groups, SUB, half), bf16),
            dma((4, CHUNKS, R)), dma((4, CHUNKS, R)), dma((4, CHUNKS, R)), dma((4, CHUNKS, R)),
            dma((4, C)), dma((4, C)), dma((4, C)), dma((4, C)),
            dma((6, 2)), dma((6, 2)), dma((3, 4)),
        ],
        compiler_params=pltpu.CompilerParams(collective_id=0, has_side_effects=True, vmem_limit_bytes=56 << 20),
    )(*views, conv_weight, jnp.transpose(row_mask, (1, 2, 0)), jnp.transpose(col_mask, (1, 2, 0)))
    split = 2
    one = pl.BlockSpec((1, groups, SUB, width // split), lambda i, j: (i, 0, 0, j))
    outs = pl.pallas_call(
        finish_kernel,
        out_shape=[jax.ShapeDtypeStruct((rows, groups, SUB, width), bf16)] * 4,
        grid=(rows, split),
        in_specs=[
            pl.BlockSpec((4, 1, groups, SUB, width // split), lambda i, j: (0, i, 0, 0, j)),
            pl.BlockSpec((2, 1, groups, SUB, width // split), lambda i, j: (0, i, 0, 0, j)),
        ],
        out_specs=[one] * 4,
    )(ret, conv)
    return tuple(x.reshape(query.shape) for x in outs)


def any_body(query, key, value, cotangent, conv_weight, row_mask, col_mask):
    rows, cols_here, width = query.shape
    R, C = lax.axis_size("rows"), lax.axis_size("cols")
    fits = R % 2 == 0 and cols_here == R * SUB and (width // 2) % (C * HEAD_DIM) == 0
    chosen = fused_body if fits else body
    return chosen(query, key, value, cotangent, conv_weight, row_mask, col_mask)


def solution(mesh):
    return jax.shard_map(
        any_body,
        mesh=mesh,
        in_specs=(
            P("rows", "cols", None),
            P("rows", "cols", None),
            P("rows", "cols", None),
            P("rows", "cols", None),
            P(),
            P("rows", None, None),
            P("cols", None, None),
        ),
        out_specs=(
            P("rows", "cols", None),
            P("rows", "cols", None),
            P("rows", "cols", None),
            P("rows", "cols", None),
        ),
        check_vma=False,
    )
```
